32 devices in a mesh: grp: 2 (over y), inner: 8 (over z, x), outer: 2 (over core).
Axes of the slice: x: 2, y: 2, z: 4, core: 2. Of those that a mesh axis runs over, the one named last changes fastest.
Arguments:
- tokens: bfloat16 [4, 6144, 4096], P(('grp', 'outer'), 'inner'), parts along dimension 0, may hold values from -6 to 6
- w_in: bfloat16 [4096, 1536], P('inner'), may hold values from -0.09375 to 0.09375
- w_dt: bfloat16 [4096, 16], P('inner'), may hold values from -0.09375 to 0.09375
- conv_w: float32 [4, 1536], replicated, may hold values from -0.6 to 0.6
- conv_b: float32 [1536], replicated, may hold values from -0.5 to 0.5
- dt_bias: float32 [16], replicated, may hold values from -2 to 0
- a_log: float32 [16], replicated
- d_skip: float32 [16], replicated, may hold values from 0.5 to 8
- norm_gain: float32 [1024], replicated, may hold values from 0.1 to 1.9
Outputs:
- mixed: bfloat16 [4, 6144, 1024], P(('grp', 'outer'), 'inner'), parts along dimension 0
- entry_states: float32 [4, 8, 16, 64, 256], P(('grp', 'outer'), 'inner'), parts along dimension 0
The draws below stay inside these ranges and needn't reach their ends.
There are 2 independent parts, one for each index of `grp`. The reference program is written for one: setup_inputs(seed, part) draws one part's arguments, and reference() takes and returns one part's arrays. A program takes and returns all parts, laid end to end along the dimension named above; an argument that names none is the same for every part. Nothing has to cross between parts.
All inputs are finite; a program needn't handle non-finite values.
Results may differ from the reference program's by a relative error of at most 0.004.
Values may be sent and summed in bfloat16 or wider, within the bound.
A program may use at most 192 MiB of HBM per device.

```python
import math
from functools import partial
import jax
import jax.numpy as jnp
from jax import lax

D = 4096
HEADS = 16
P_SIZE = 64
N = 256
CONV = 4
TOK_DEV = 768
HP = 1024
XBC = 1536
BLOCKS = 2
SPANS = 8
BLOCK_LEN = 6144


def draw_a_log(key, part):
    chain_len = BLOCKS * BLOCK_LEN
    slowest = jnp.log(0.25 / chain_len)
    fastest = jnp.log(1.0 / 30.0)
    first_key = jax.random.fold_in(key, 0)
    spread = jax.random.uniform(first_key, (HEADS,), jnp.float32)
    return jnp.log(2.5) + slowest + spread * (fastest - slowest)


def levels(own_key, shape, cuts, smallest, high):
    loudness, own = 1.0, jax.random.fold_in(own_key, 6)
    for axis_at, parts in cuts:
        draws = jnp.exp(jax.random.uniform(jax.random.fold_in(own, axis_at), (parts,), jnp.float32, smallest / len(cuts), high / len(cuts)))
        loudness = loudness * jnp.repeat(draws, shape[axis_at] // parts).reshape([-1 if axis == axis_at else 1 for axis in range(len(shape))])
    return loudness


def bell_draw(stream_key, dims, scale, reach, pieces=(), held_as=jnp.bfloat16):
    values = jax.random.normal(stream_key, dims, jnp.float32) * scale
    if len(pieces) > 0:
        values = levels(stream_key, dims, pieces, -0.22, 0.18) * values
    return jnp.clip(values, min=-reach, max=reach).astype(held_as)


def setup_inputs(seed: int = 0, part: int = 0) -> dict:
    arg_keys = jax.random.split(jax.random.key(seed), 10)
    own_keys = jax.random.split(jax.random.fold_in(arg_keys[9], part), 10)
    tokens = bell_draw(own_keys[0], (BLOCKS, BLOCK_LEN, D), 1.0, 6.0, ((0, 2), (1, 8)))
    w_in = bell_draw(arg_keys[1], (D, XBC), D ** -0.5, 0.09375, ((0, 8),))
    w_dt = bell_draw(arg_keys[2], (D, HEADS), D ** -0.5, 0.09375, ((0, 8),))
    conv_w = jnp.clip(jax.random.uniform(arg_keys[3], (CONV, XBC), jnp.float32, -0.6, 0.6), -0.6, 0.6)
    conv_b = jnp.clip(jax.random.uniform(arg_keys[4], (XBC,), jnp.float32, -0.5, 0.5), -0.5, 0.5)
    dt_bias = jnp.clip(jax.random.uniform(arg_keys[5], (HEADS,), jnp.float32, -2.0, 0.0), -2.0, 0.0)
    a_log = draw_a_log(jax.random.fold_in(arg_keys[9], 71), part)
    d_skip = jnp.clip(jnp.exp(jax.random.uniform(arg_keys[7], (HEADS,), jnp.float32, math.log(0.5), math.log(8.0))), 0.5, 8.0)
    norm_gain = jnp.clip(1.0 + 0.18 * jax.random.normal(arg_keys[8], (HP,), jnp.float32), 0.1, 1.9)
    return dict(tokens=tokens, w_in=w_in, w_dt=w_dt, conv_w=conv_w, conv_b=conv_b, dt_bias=dt_bias, a_log=a_log, d_skip=d_skip, norm_gain=norm_gain)


EPSILON = 1e-05

def rounded(values):
    return lax.optimization_barrier(values.astype(jnp.bfloat16)).astype(jnp.float32)

def prepare_span(projected, dt_raw, tail_rows, conv_w, conv_b, dt_bias, a_log):
    length = projected.shape[0]
    padded = jnp.concatenate([tail_rows, projected], axis=0).astype(jnp.float32)
    conv_sum = conv_b[None, :] + conv_w[0][None, :] * padded[0:length]
    for offset in range(1, CONV):
        conv_sum = conv_sum + conv_w[offset][None, :] * padded[offset:offset + length]
    conv_out = jax.nn.silu(conv_sum).astype(jnp.bfloat16)
    inputs = conv_out[:, :HEADS * P_SIZE].reshape(length, HEADS, P_SIZE).transpose(1, 0, 2)
    b_rows = conv_out[:, HEADS * P_SIZE:HEADS * P_SIZE + N]
    c_rows = conv_out[:, HEADS * P_SIZE + N:]
    step_size = jax.nn.softplus(dt_raw.astype(jnp.float32) + dt_bias[None, :]).T
    log_decay = jnp.cumsum(step_size * (-jnp.exp(a_log))[:, None], axis=1)
    return (inputs, b_rows, c_rows, step_size, log_decay)

def span_state(inputs, b_rows, step_size, log_decay):
    final_log = log_decay[:, -1:]
    weighted = rounded((jnp.exp(final_log - log_decay) * step_size)[:, :, None] * inputs.astype(jnp.float32))
    contrib = jnp.einsum('hqp,qn->hpn', weighted, b_rows.astype(jnp.float32))
    return (jnp.exp(log_decay[:, -1]), contrib)

def head_rows(c_rows, scores, operands):
    log_h, input_h, step_h, entry_h, skip_h, gain_h = operands
    length = log_h.shape[0]
    row_ids = lax.broadcasted_iota(jnp.int32, (length, length), 0)
    col_ids = lax.broadcasted_iota(jnp.int32, (length, length), 1)
    causal = col_ids <= row_ids
    log_gap = jnp.where(causal, log_h[:, None] - log_h[None, :], 0.0)
    mixing = jnp.where(causal, scores * jnp.exp(log_gap), 0.0).astype(jnp.bfloat16)
    driven = (step_h[:, None] * input_h.astype(jnp.float32)).astype(jnp.bfloat16)
    output = jnp.dot(mixing, driven, preferred_element_type=jnp.float32)
    carried = jnp.dot(c_rows, entry_h.astype(jnp.bfloat16).T, preferred_element_type=jnp.float32)
    output = output + jnp.exp(log_h)[:, None] * carried + skip_h * input_h.astype(jnp.float32)
    inv_rms = lax.rsqrt(lax.optimization_barrier(jnp.mean(output * output, axis=1, keepdims=True)) + EPSILON)
    return output * inv_rms * gain_h[None, :]

def span_output(inputs, b_rows, c_rows, step_size, log_decay, entry_state, d_skip, norm_gain):
    scores = jnp.dot(c_rows, b_rows.T, preferred_element_type=jnp.float32)
    head_gains = norm_gain.reshape(HEADS, P_SIZE)
    per_head = lax.map(partial(head_rows, c_rows, scores), (log_decay, inputs, step_size, entry_state, d_skip, head_gains))
    return per_head.transpose(1, 0, 2).reshape(inputs.shape[1], HEADS * P_SIZE).astype(jnp.bfloat16)

def reference(tokens, w_in, w_dt, conv_w, conv_b, dt_bias, a_log, d_skip, norm_gain):
    ranges = tokens.reshape(BLOCKS * SPANS, TOK_DEV, D)
    start_state = jnp.zeros((HEADS, P_SIZE, N), jnp.float32)
    start_tail = jnp.zeros((CONV - 1, HEADS * P_SIZE + 2 * N), jnp.bfloat16)

    def advance(carried_in, token_block):
        current, tail_rows = carried_in
        projected = jnp.dot(token_block, w_in, preferred_element_type=jnp.float32).astype(jnp.bfloat16)
        dt_raw = jnp.dot(token_block, w_dt, preferred_element_type=jnp.float32).astype(jnp.bfloat16)
        inputs, b_rows, c_rows, step_size, log_decay = prepare_span(projected, dt_raw, tail_rows, conv_w, conv_b, dt_bias, a_log)
        decay_total, contrib = span_state(inputs, b_rows, step_size, log_decay)
        output = span_output(inputs, b_rows, c_rows, step_size, log_decay, current, d_skip, norm_gain)
        next_state = decay_total[:, None, None] * current + contrib
        return ((next_state, projected[TOK_DEV - CONV + 1:]), (output, current))
    last_carry, stacked = lax.scan(advance, (start_state, start_tail), ranges)
    outputs, entries = stacked
    return (outputs.reshape(BLOCKS, BLOCK_LEN, HEADS * P_SIZE), entries.reshape(BLOCKS, SPANS, HEADS, P_SIZE, N))
```

```python
from functools import partial

import jax
import jax.numpy as jnp
from jax import lax
from jax.experimental import pallas as pl
from jax.experimental.pallas import tpu as pltpu
from jax.sharding import PartitionSpec as P

HEADS = 16
P_SIZE = 64
N = 256
CONV = 4
HP = HEADS * P_SIZE
CHUNK = 256
EPSILON = 1e-05
MESH = pl.DeviceIdType.MESH
F32 = jnp.float32
BF16 = jnp.bfloat16
LAST = (((1,), (1,)), ((), ()))
FIRST = (((0,), (0,)), ((), ()))


def expand(values, spread):
    high = values.astype(BF16)
    low = (values - high.astype(F32)).astype(BF16)
    return jnp.dot(high, spread, preferred_element_type=F32) + jnp.dot(
        low, spread, preferred_element_type=F32
    )


def scan_kernel(
    n_in, ndev,
    proj, tail, dt_raw, conv_w, conv_b, dt_bias, a_log, d_skip, gain,
    mixed, entry_out,
    pad, conv, log_s, log_t, step_s, y, states,
    send1, recv1, send2, recv2, dec_send, dec_recv,
    ss1, rs1, ss2, rs2, ssd, rsd,
):
    length = proj.shape[0]
    chunks = length // CHUNK
    rows = HP // ndev
    me = lax.axis_index("outer") * n_in + lax.axis_index("inner")

    def place(g):
        return {"inner": lax.rem(g, n_in), "outer": lax.div(g, n_in)}

    barrier = pltpu.get_barrier_semaphore()

    def greet(k, carry):
        pl.semaphore_signal(
            barrier, inc=1, device_id=place(lax.rem(me + k, ndev)), device_id_type=MESH
        )
        return carry

    lax.fori_loop(1, ndev, greet, 0)

    head_id = lax.broadcasted_iota(jnp.int32, (HEADS, HP), 0)
    col_head = lax.broadcasted_iota(jnp.int32, (HEADS, HP), 1) // P_SIZE
    spread = (head_id == col_head).astype(F32).astype(BF16)

    step_size = jax.nn.softplus(dt_raw[...].astype(F32) + dt_bias[...])
    scaled = step_size * (-jnp.exp(a_log[...]))
    row_id = lax.broadcasted_iota(jnp.int32, (CHUNK, CHUNK), 0)
    col_id = lax.broadcasted_iota(jnp.int32, (CHUNK, CHUNK), 1)
    causal = col_id <= row_id
    lower = causal.astype(F32)
    step_s[...] = step_size
    before = jnp.zeros((1, HEADS), F32)
    for c in range(chunks):
        part = jnp.dot(
            lower,
            scaled[c * CHUNK : (c + 1) * CHUNK],
            preferred_element_type=F32,
            precision=lax.Precision.HIGHEST,
        ) + before
        log_s[c * CHUNK : (c + 1) * CHUNK] = part
        before = part[CHUNK - 1 : CHUNK]
    log_t[...] = jnp.transpose(log_s[...])
    dec_send[...] = jnp.broadcast_to(jnp.exp(log_t[:, length - 1 : length]), (HEADS, 128))

    pad[0:8] = tail[...].astype(F32)
    pad[8:] = proj[...].astype(F32)
    wide = 256
    blocks = proj.shape[1] // wide

    def conv_block(t, carry):
        i, j = lax.div(t, blocks), lax.rem(t, blocks)
        cols = pl.ds(pl.multiple_of(j * wide, wide), wide)
        window = pad[pl.ds(pl.multiple_of(i * 128, 128), 136), cols]
        total = conv_b[:, cols]
        for k in range(CONV):
            total = total + conv_w[k : k + 1, cols] * window[5 + k : 5 + k + 128]
        conv[pl.ds(pl.multiple_of(i * 128, 128), 128), cols] = (
            total * jax.nn.sigmoid(total)
        ).astype(BF16)
        return carry

    lax.fori_loop(0, (length // 128) * blocks, conv_block, 0)

    def weighted_sum(stop):
        final = log_s[stop - 1 : stop]
        factor = jnp.exp(final - log_s[0:stop]) * step_s[0:stop]
        weighted = (expand(factor, spread) * conv[0:stop, 0:HP].astype(F32)).astype(BF16)
        return lax.dot_general(
            weighted, conv[0:stop, HP : HP + N], FIRST, preferred_element_type=F32
        )

    send1[...] = weighted_sum(length).reshape(ndev, rows, N).astype(BF16)
    recv1[me] = send1[me]
    dec_recv[me] = dec_send[...]

    def decay_copy(g):
        return pltpu.make_async_remote_copy(
            src_ref=dec_send, dst_ref=dec_recv.at[me], send_sem=ssd.at[g],
            recv_sem=rsd.at[me], device_id=place(g), device_id_type=MESH,
        )

    def first_copy(g):
        return pltpu.make_async_remote_copy(
            src_ref=send1.at[g], dst_ref=recv1.at[me], send_sem=ss1.at[g],
            recv_sem=rs1.at[me], device_id=place(g), device_id_type=MESH,
        )

    def second_copy(g):
        return pltpu.make_async_remote_copy(
            src_ref=send2.at[g], dst_ref=recv2.at[me], send_sem=ss2.at[g],
            recv_sem=rs2.at[me], device_id=place(g), device_id_type=MESH,
        )

    pl.semaphore_wait(barrier, ndev - 1)

    def send_first(k, carry):
        g = lax.rem(me + k, ndev)
        decay_copy(g).start()
        first_copy(g).start()
        return carry

    lax.fori_loop(1, ndev, send_first, 0)

    states[0] = jnp.zeros((HP, N), BF16)
    for c in range(1, chunks):
        states[c] = weighted_sum(c * CHUNK).astype(BF16)

    def local_chunk(c, carry):
        start = pl.multiple_of(c * CHUNK, CHUNK)
        here = pl.ds(start, CHUNK)
        log_c = log_s[here]
        reached = log_s[pl.ds(pl.multiple_of(jnp.maximum(start - 8, 0), 8), 8)][7:8]
        reached = jnp.where(c > 0, reached, 0.0)
        c_rows = conv[here, HP + N :]
        b_rows = conv[here, HP : HP + N]
        scores = lax.dot_general(c_rows, b_rows, LAST, preferred_element_type=F32)
        scores = jnp.where(causal, scores, 0.0)
        x_rows = conv[here, 0:HP].astype(F32)
        driven = (expand(step_s[here], spread) * x_rows).astype(BF16)
        inter = lax.dot_general(c_rows, states[c], LAST, preferred_element_type=F32)
        y[here] = expand(jnp.exp(log_c - reached), spread) * inter + d_skip[...] * x_rows
        for h in range(0, HEADS, 2):
            pieces = []
            for k in (h, h + 1):
                gap = jnp.minimum(log_c[:, k : k + 1] - log_t[k : k + 1, here], 0.0)
                mixing = (scores * jnp.exp(gap)).astype(BF16)
                pieces.append(
                    jnp.dot(
                        mixing,
                        driven[:, k * P_SIZE : (k + 1) * P_SIZE],
                        preferred_element_type=F32,
                    )
                )
            both = slice(h * P_SIZE, (h + 2) * P_SIZE)
            y[here, both] = y[here, both] + jnp.concatenate(pieces, axis=1)
        return carry

    lax.fori_loop(0, chunks, local_chunk, 0)

    own_head = lax.div(me * rows, P_SIZE)

    def wait_from(copy_of, r):
        copy_of(r).wait_recv()

    def arrive(buffer, sems, r):
        pltpu.make_async_remote_copy(
            src_ref=buffer.at[r], dst_ref=buffer.at[r], send_sem=sems.at[r],
            recv_sem=sems.at[r], device_id=place(r), device_id_type=MESH,
        ).wait_recv()

    def advance(r, state):
        send2[r] = state.astype(BF16)

        @pl.when(r != me)
        def _():
            second_copy(r).start()
            arrive(dec_recv, rsd, r)
            arrive(recv1, rs1, r)

        decay = dec_recv[r, pl.ds(own_head, 1), :]
        decay = jnp.concatenate([decay, decay], axis=1)
        return decay * state + recv1[r].astype(F32)

    lax.fori_loop(0, ndev, advance, jnp.zeros((rows, N), F32))
    recv2[me] = send2[me]

    def finish(k, carry):
        g = lax.rem(me + k, ndev)
        arrive(recv2, rs2, g)
        decay_copy(g).wait_send()
        first_copy(g).wait_send()
        second_copy(g).wait_send()
        return carry

    lax.fori_loop(1, ndev, finish, 0)

    entry = recv2[...].astype(F32).reshape(HP, N)
    entry_out[...] = entry
    entry = entry.astype(BF16)
    for c in range(chunks):
        here = slice(c * CHUNK, (c + 1) * CHUNK)
        carried = lax.dot_general(
            conv[here, HP + N :], entry, LAST, preferred_element_type=F32
        )
        out = y[here] + expand(jnp.exp(log_s[here]), spread) * carried
        square = out * out
        high = square.astype(BF16)
        low = (square - high.astype(F32)).astype(BF16)
        sums = lax.dot_general(high, spread, LAST, preferred_element_type=F32)
        sums = sums + lax.dot_general(low, spread, LAST, preferred_element_type=F32)
        inv_rms = lax.rsqrt(sums * (1.0 / P_SIZE) + EPSILON)
        mixed[here] = (out * expand(inv_rms, spread) * gain[...]).astype(BF16)


def run_scan(projected, tail, dt_raw, conv_w, conv_b, dt_bias, a_log, d_skip, norm_gain):
    n_in, n_out = lax.axis_size("inner"), lax.axis_size("outer")
    ndev = n_in * n_out
    length, xbc = projected.shape
    rows = HP // ndev
    dma = pltpu.SemaphoreType.DMA((ndev,))
    vmem = pl.BlockSpec(memory_space=pltpu.VMEM)
    return pl.pallas_call(
        partial(scan_kernel, n_in, ndev),
        out_shape=(
            jax.ShapeDtypeStruct((length, HP), BF16),
            jax.ShapeDtypeStruct((HP, N), F32),
        ),
        in_specs=[vmem] * 9,
        out_specs=(vmem, vmem),
        scratch_shapes=[
            pltpu.VMEM((length + 8, xbc), F32),
            pltpu.VMEM((length, xbc), BF16),
            pltpu.VMEM((length, HEADS), F32),
            pltpu.VMEM((HEADS, length), F32),
            pltpu.VMEM((length, HEADS), F32),
            pltpu.VMEM((length, HP), F32),
            pltpu.VMEM((length // CHUNK, HP, N), BF16),
            pltpu.VMEM((ndev, rows, N), BF16),
            pltpu.VMEM((ndev, rows, N), BF16),
            pltpu.VMEM((ndev, rows, N), BF16),
            pltpu.VMEM((ndev, rows, N), BF16),
            pltpu.VMEM((HEADS, 128), F32),
            pltpu.VMEM((ndev, HEADS, 128), F32),
            dma, dma, dma, dma, dma, dma,
        ],
        compiler_params=pltpu.CompilerParams(
            collective_id=1, has_side_effects=True, vmem_limit_bytes=60 * 2**20
        ),
        name="scan",
    )(
        projected, tail, dt_raw, conv_w, conv_b[None, :], dt_bias[None, :], a_log[None, :],
        jnp.repeat(d_skip, P_SIZE)[None, :], norm_gain[None, :],
    )


def per_device(tokens, w_in, w_dt, conv_w, conv_b, dt_bias, a_log, d_skip, norm_gain):
    own_rows = tokens.reshape(tokens.shape[1], tokens.shape[2])
    row_count = own_rows.shape[0]
    n_in, n_out = lax.axis_size("inner"), lax.axis_size("outer")
    full_x = lax.all_gather(w_in, "inner", axis=0, tiled=True)
    full_dt = lax.all_gather(w_dt, "inner", axis=0, tiled=True)
    projected = jnp.dot(own_rows, full_x, preferred_element_type=F32).astype(BF16)
    dt_raw = jnp.dot(own_rows, full_dt, preferred_element_type=F32).astype(BF16)
    order = [(r, r + 1) for r in range(n_in * n_out - 1)]
    pairs = [((r % n_in) * n_out + r // n_in, (s % n_in) * n_out + s // n_in) for r, s in order]
    tail = lax.ppermute(projected[row_count - 8 :], ("inner", "outer"), pairs)
    mixed, entry = run_scan(
        projected, tail, dt_raw, conv_w, conv_b, dt_bias, a_log, d_skip, norm_gain
    )
    return (
        mixed.reshape(1, row_count, HP),
        entry.reshape(1, 1, HEADS, P_SIZE, N),
    )


def solution(mesh):
    placed = (
        P(("grp", "outer"), "inner", None),
        P("inner", None),
        P("inner", None),
        P(), P(), P(), P(), P(), P(),
    )
    return jax.shard_map(
        per_device,
        mesh=mesh,
        in_specs=placed,
        out_specs=(
            P(("grp", "outer"), "inner", None),
            P(("grp", "outer"), "inner", None, None, None),
        ),
        check_vma=False,
    )
```

```python
from functools import partial

import jax
import jax.numpy as jnp
from jax import lax
from jax.experimental import pallas as pl
from jax.experimental.pallas import tpu as pltpu
from jax.sharding import PartitionSpec as P

HEADS = 16
P_SIZE = 64
N = 256
CONV = 4
HP = HEADS * P_SIZE
CHUNK = 256
EPSILON = 1e-05
MESH = pl.DeviceIdType.MESH
F32 = jnp.float32
BF16 = jnp.bfloat16
LAST = (((1,), (1,)), ((), ()))
FIRST = (((0,), (0,)), ((), ()))


def expand(values, spread):
    high = values.astype(BF16)
    low = (values - high.astype(F32)).astype(BF16)
    return jnp.dot(high, spread, preferred_element_type=F32) + jnp.dot(
        low, spread, preferred_element_type=F32
    )


def scan_kernel(
    n_in, ndev,
    proj, tail, dt_raw, conv_w, conv_b, dt_bias, a_log, d_skip, gain,
    mixed, entry_out,
    pad, conv, log_s, log_t, step_s, y, states,
    send1, recv1, send2, recv2, dec_send, dec_recv,
    ss1, rs1, ss2, rs2, ssd, rsd,
):
    length = proj.shape[0]
    chunks = length // CHUNK
    rows = HP // ndev
    me = lax.axis_index("outer") * n_in + lax.axis_index("inner")

    def place(g):
        return {"inner": lax.rem(g, n_in), "outer": lax.div(g, n_in)}

    barrier = pltpu.get_barrier_semaphore()

    def greet(k, carry):
        pl.semaphore_signal(
            barrier, inc=1, device_id=place(lax.rem(me + k, ndev)), device_id_type=MESH
        )
        return carry

    lax.fori_loop(1, ndev, greet, 0)

    head_id = lax.broadcasted_iota(jnp.int32, (HEADS, HP), 0)
    col_head = lax.broadcasted_iota(jnp.int32, (HEADS, HP), 1) // P_SIZE
    spread = (head_id == col_head).astype(F32).astype(BF16)

    step_size = jax.nn.softplus(dt_raw[...].astype(F32) + dt_bias[...])
    scaled = step_size * (-jnp.exp(a_log[...]))
    row_id = lax.broadcasted_iota(jnp.int32, (CHUNK, CHUNK), 0)
    col_id = lax.broadcasted_iota(jnp.int32, (CHUNK, CHUNK), 1)
    causal = col_id <= row_id
    lower = causal.astype(F32)
    step_s[...] = step_size
    before = jnp.zeros((1, HEADS), F32)
    for c in range(chunks):
        part = jnp.dot(
            lower,
            scaled[c * CHUNK : (c + 1) * CHUNK],
            preferred_element_type=F32,
            precision=lax.Precision.HIGHEST,
        ) + before
        log_s[c * CHUNK : (c + 1) * CHUNK] = part
        before = part[CHUNK - 1 : CHUNK]
    log_t[...] = jnp.transpose(log_s[...])
    dec_send[...] = jnp.broadcast_to(jnp.exp(log_t[:, length - 1 : length]), (HEADS, 128))

    pad[0:8] = tail[...].astype(F32)[8:16]
    pad[8:] = proj[...].astype(F32)
    wide = 256
    blocks = proj.shape[1] // wide

    def conv_block(t, carry):
        i, j = lax.div(t, blocks), lax.rem(t, blocks)
        cols = pl.ds(pl.multiple_of(j * wide, wide), wide)
        window = pad[pl.ds(pl.multiple_of(i * 128, 128), 136), cols]
        total = conv_b[:, cols]
        for k in range(CONV):
            total = total + conv_w[k : k + 1, cols] * window[5 + k : 5 + k + 128]
        conv[pl.ds(pl.multiple_of(i * 128, 128), 128), cols] = (
            total * jax.nn.sigmoid(total)
        ).astype(BF16)
        return carry

    lax.fori_loop(0, (length // 128) * blocks, conv_block, 0)

    def weighted_sum(stop):
        final = log_s[stop - 1 : stop]
        factor = jnp.exp(final - log_s[0:stop]) * step_s[0:stop]
        weighted = (expand(factor, spread) * conv[0:stop, 0:HP].astype(F32)).astype(BF16)
        return lax.dot_general(
            weighted, conv[0:stop, HP : HP + N], FIRST, preferred_element_type=F32
        )

    send1[...] = weighted_sum(length).reshape(ndev, rows, N).astype(BF16)
    recv1[me] = send1[me]
    dec_recv[me] = dec_send[...]

    def decay_copy(g):
        return pltpu.make_async_remote_copy(
            src_ref=dec_send, dst_ref=dec_recv.at[me], send_sem=ssd.at[g],
            recv_sem=rsd.at[me], device_id=place(g), device_id_type=MESH,
        )

    def first_copy(g):
        return pltpu.make_async_remote_copy(
            src_ref=send1.at[g], dst_ref=recv1.at[me], send_sem=ss1.at[g],
            recv_sem=rs1.at[me], device_id=place(g), device_id_type=MESH,
        )

    def second_copy(g):
        return pltpu.make_async_remote_copy(
            src_ref=send2.at[g], dst_ref=recv2.at[me], send_sem=ss2.at[g],
            recv_sem=rs2.at[me], device_id=place(g), device_id_type=MESH,
        )

    pl.semaphore_wait(barrier, ndev - 1)

    def send_first(k, carry):
        g = lax.rem(me + k, ndev)
        decay_copy(g).start()
        first_copy(g).start()
        return carry

    lax.fori_loop(1, ndev, send_first, 0)

    states[0] = jnp.zeros((HP, N), BF16)
    for c in range(1, chunks):
        states[c] = weighted_sum(c * CHUNK).astype(BF16)

    def local_chunk(c, carry):
        start = pl.multiple_of(c * CHUNK, CHUNK)
        here = pl.ds(start, CHUNK)
        log_c = log_s[here]
        reached = log_s[pl.ds(pl.multiple_of(jnp.maximum(start - 8, 0), 8), 8)][7:8]
        reached = jnp.where(c > 0, reached, 0.0)
        c_rows = conv[here, HP + N :]
        b_rows = conv[here, HP : HP + N]
        scores = lax.dot_general(c_rows, b_rows, LAST, preferred_element_type=F32)
        scores = jnp.where(causal, scores, 0.0)
        x_rows = conv[here, 0:HP].astype(F32)
        driven = (expand(step_s[here], spread) * x_rows).astype(BF16)
        inter = lax.dot_general(c_rows, states[c], LAST, preferred_element_type=F32)
        y[here] = expand(jnp.exp(log_c - reached), spread) * inter + d_skip[...] * x_rows
        for h in range(0, HEADS, 2):
            pieces = []
            for k in (h, h + 1):
                gap = jnp.minimum(log_c[:, k : k + 1] - log_t[k : k + 1, here], 0.0)
                mixing = (scores * jnp.exp(gap)).astype(BF16)
                pieces.append(
                    jnp.dot(
                        mixing,
                        driven[:, k * P_SIZE : (k + 1) * P_SIZE],
                        preferred_element_type=F32,
                    )
                )
            both = slice(h * P_SIZE, (h + 2) * P_SIZE)
            y[here, both] = y[here, both] + jnp.concatenate(pieces, axis=1)
        return carry

    lax.fori_loop(0, chunks, local_chunk, 0)

    own_head = lax.div(me * rows, P_SIZE)

    def wait_from(copy_of, r):
        copy_of(r).wait_recv()

    def arrive(buffer, sems, r):
        pltpu.make_async_remote_copy(
            src_ref=buffer.at[r], dst_ref=buffer.at[r], send_sem=sems.at[r],
            recv_sem=sems.at[r], device_id=place(r), device_id_type=MESH,
        ).wait_recv()

    def advance(r, state):
        send2[r] = state.astype(BF16)

        @pl.when(r != me)
        def _():
            second_copy(r).start()
            arrive(dec_recv, rsd, r)
            arrive(recv1, rs1, r)

        decay = dec_recv[r, pl.ds(own_head, 1), :]
        decay = jnp.concatenate([decay, decay], axis=1)
        return decay * state + recv1[r].astype(F32)

    lax.fori_loop(0, ndev, advance, jnp.zeros((rows, N), F32))
    recv2[me] = send2[me]

    def finish(k, carry):
        g = lax.rem(me + k, ndev)
        arrive(recv2, rs2, g)
        decay_copy(g).wait_send()
        first_copy(g).wait_send()
        second_copy(g).wait_send()
        return carry

    lax.fori_loop(1, ndev, finish, 0)

    entry = recv2[...].astype(F32).reshape(HP, N)
    entry_out[...] = entry
    entry = entry.astype(BF16)
    for c in range(chunks):
        here = slice(c * CHUNK, (c + 1) * CHUNK)
        carried = lax.dot_general(
            conv[here, HP + N :], entry, LAST, preferred_element_type=F32
        )
        out = y[here] + expand(jnp.exp(log_s[here]), spread) * carried
        square = out * out
        high = square.astype(BF16)
        low = (square - high.astype(F32)).astype(BF16)
        sums = lax.dot_general(high, spread, LAST, preferred_element_type=F32)
        sums = sums + lax.dot_general(low, spread, LAST, preferred_element_type=F32)
        inv_rms = lax.rsqrt(sums * (1.0 / P_SIZE) + EPSILON)
        mixed[here] = (out * expand(inv_rms, spread) * gain[...]).astype(BF16)


def run_scan(projected, tail, dt_raw, conv_w, conv_b, dt_bias, a_log, d_skip, norm_gain):
    n_in, n_out = lax.axis_size("inner"), lax.axis_size("outer")
    ndev = n_in * n_out
    length, xbc = projected.shape
    rows = HP // ndev
    dma = pltpu.SemaphoreType.DMA((ndev,))
    vmem = pl.BlockSpec(memory_space=pltpu.VMEM)
    return pl.pallas_call(
        partial(scan_kernel, n_in, ndev),
        out_shape=(
            jax.ShapeDtypeStruct((length, HP), BF16),
            jax.ShapeDtypeStruct((HP, N), F32),
        ),
        in_specs=[vmem] * 9,
        out_specs=(vmem, vmem),
        scratch_shapes=[
            pltpu.VMEM((length + 8, xbc), F32),
            pltpu.VMEM((length, xbc), BF16),
            pltpu.VMEM((length, HEADS), F32),
            pltpu.VMEM((HEADS, length), F32),
            pltpu.VMEM((length, HEADS), F32),
            pltpu.VMEM((length, HP), F32),
            pltpu.VMEM((length // CHUNK, HP, N), BF16),
            pltpu.VMEM((ndev, rows, N), BF16),
            pltpu.VMEM((ndev, rows, N), BF16),
            pltpu.VMEM((ndev, rows, N), BF16),
            pltpu.VMEM((ndev, rows, N), BF16),
            pltpu.VMEM((HEADS, 128), F32),
            pltpu.VMEM((ndev, HEADS, 128), F32),
            dma, dma, dma, dma, dma, dma,
        ],
        compiler_params=pltpu.CompilerParams(
            collective_id=1, has_side_effects=True, vmem_limit_bytes=60 * 2**20
        ),
        name="scan",
    )(
        projected, tail, dt_raw, conv_w, conv_b[None, :], dt_bias[None, :], a_log[None, :],
        jnp.repeat(d_skip, P_SIZE)[None, :], norm_gain[None, :],
    )


def project_kernel(
    n, n_out,
    tokens, w_in, w_dt,
    proj, tail, dt_out,
    tok, held, total, held_dt,
    ring_s, ring_r, side_s, side_r, core_s, core_r, dt_s, dt_r, misc, tail_s, tail_r,
):
    length, depth = tokens.shape
    local, xbc = w_in.shape
    half = xbc // 2
    quarter = half // 2
    lanes = 128
    streams = quarter // lanes
    wide = 256
    tiles = half // wide
    third = (local * 5 // 16) // 16 * 16
    ring_rows = local - third
    tail_rows = tok.shape[0] - length
    block = held_dt.shape[2]
    ndev = n * n_out
    me = lax.axis_index("inner")
    core = lax.axis_index("outer")
    grp = lax.axis_index("grp")
    rank = core * n + me
    odd = lax.rem(me, 2)
    pos = jnp.where(odd == 0, lax.div(me, 2), n - lax.div(me + 1, 2))

    def index_at(q):
        q = lax.rem(q + 2 * n, n)
        return jnp.where(q < n // 2, 2 * q, 2 * n - 1 - 2 * q)

    def place(g):
        return {"inner": lax.rem(g, n), "outer": lax.div(g, n)}

    barrier = pltpu.get_barrier_semaphore()

    def greet(k, carry):
        pl.semaphore_signal(
            barrier, inc=1, device_id=place(lax.rem(rank + k, ndev)), device_id_type=MESH
        )
        return carry

    lax.fori_loop(1, ndev, greet, 0)
    pl.semaphore_signal(barrier, inc=1, device_id={"grp": 1 - grp}, device_id_type=MESH)

    def own_rows(owner):
        return pl.ds(pl.multiple_of(owner * local, 16), local)

    load_tok = pltpu.make_async_copy(tokens, tok.at[pl.ds(0, length)], misc.at[0])
    load_w = [
        pltpu.make_async_copy(
            w_in.at[:, pl.ds(d * half, half)], held.at[d, own_rows(me)], misc.at[1 + d]
        )
        for d in range(2)
    ]
    for copy in load_w:
        copy.start()
    load_tok.start()
    held_dt[me] = w_dt[...]

    @pl.when(rank == 0)
    def _():
        tok[length:] = jnp.zeros((tail_rows, depth), BF16)

    def ring_copy(d, t, s):
        owner = index_at(pos - (s - 1)) if d == 0 else index_at(pos + (s - 1))
        target = index_at(pos + 1) if d == 0 else index_at(pos - 1)
        rows = pl.ds(pl.multiple_of(owner * local + grp * third, 16), ring_rows)
        cols = pl.ds(pl.multiple_of(core * quarter + t * lanes, lanes), lanes)
        part = held.at[d, rows, cols]
        return pltpu.make_async_remote_copy(
            src_ref=part, dst_ref=part, send_sem=ring_s.at[d, t, s],
            recv_sem=ring_r.at[d, t, s], device_id={"inner": target}, device_id_type=MESH,
        )

    def owner_of(d, s):
        return index_at(pos - s) if d == 0 else index_at(pos + s)

    def side_copy(d, s):
        rows = pl.ds(
            pl.multiple_of(owner_of(d, s) * local + grp * ring_rows, 16), third
        )
        cols = pl.ds(pl.multiple_of(core * quarter, lanes), quarter)
        part = held.at[d, rows, cols]
        return pltpu.make_async_remote_copy(
            src_ref=part, dst_ref=part, send_sem=side_s.at[d, s],
            recv_sem=side_r.at[d, s], device_id={"grp": 1 - grp}, device_id_type=MESH,
        )

    def core_copy(d, s):
        cols = pl.ds(pl.multiple_of(core * quarter, lanes), quarter)
        part = held.at[d, own_rows(owner_of(d, s)), cols]
        return pltpu.make_async_remote_copy(
            src_ref=part, dst_ref=part, send_sem=core_s.at[d, s],
            recv_sem=core_r.at[d, s], device_id={"outer": 1 - core}, device_id_type=MESH,
        )

    def ring_arrival(d, t, s):
        owner = owner_of(d, s)
        rows = pl.ds(pl.multiple_of(owner * local + grp * third, 16), ring_rows)
        cols = pl.ds(pl.multiple_of(core * quarter + t * lanes, lanes), lanes)
        part = held.at[d, rows, cols]
        pltpu.make_async_remote_copy(
            src_ref=part, dst_ref=part, send_sem=ring_s.at[d, t, s],
            recv_sem=ring_r.at[d, t, s], device_id={"inner": index_at(pos + 1)},
            device_id_type=MESH,
        ).wait_recv()

    def side_arrival(d, s):
        rows = pl.ds(
            pl.multiple_of(owner_of(d, s) * local + (1 - grp) * ring_rows, 16), third
        )
        cols = pl.ds(pl.multiple_of(core * quarter, lanes), quarter)
        part = held.at[d, rows, cols]
        pltpu.make_async_remote_copy(
            src_ref=part, dst_ref=part, send_sem=side_s.at[d, s],
            recv_sem=side_r.at[d, s], device_id={"grp": 1 - grp}, device_id_type=MESH,
        ).wait_recv()

    def core_arrival(d, s):
        cols = pl.ds(pl.multiple_of((1 - core) * quarter, lanes), quarter)
        part = held.at[d, own_rows(owner_of(d, s)), cols]
        pltpu.make_async_remote_copy(
            src_ref=part, dst_ref=part, send_sem=core_s.at[d, s],
            recv_sem=core_r.at[d, s], device_id={"outer": 1 - core}, device_id_type=MESH,
        ).wait_recv()

    def dt_copy(k):
        peer = lax.rem(me + k, n)
        return pltpu.make_async_remote_copy(
            src_ref=w_dt, dst_ref=held_dt.at[me], send_sem=dt_s.at[k],
            recv_sem=dt_r.at[me], device_id={"inner": peer}, device_id_type=MESH,
        )

    def dt_arrival(k):
        peer = lax.rem(me + k, n)
        pltpu.make_async_remote_copy(
            src_ref=w_dt, dst_ref=held_dt.at[peer], send_sem=dt_s.at[k],
            recv_sem=dt_r.at[peer], device_id={"inner": peer}, device_id_type=MESH,
        ).wait_recv()

    def tail_copy():
        return pltpu.make_async_remote_copy(
            src_ref=tokens.at[pl.ds(length - tail_rows, tail_rows)],
            dst_ref=tok.at[pl.ds(length, tail_rows)], send_sem=tail_s,
            recv_sem=tail_r, device_id=place(lax.rem(rank + 1, ndev)), device_id_type=MESH,
        )

    pl.semaphore_wait(barrier, ndev)

    @pl.when(rank < ndev - 1)
    def _():
        tail_copy().start()

    for d in range(2):
        load_w[d].wait()
        for t in range(streams):
            ring_copy(d, t, 1).start()

    def send_dt(k, carry):
        dt_copy(k).start()
        return carry

    lax.fori_loop(1, n, send_dt, 0)
    load_tok.wait()

    @pl.when(rank > 0)
    def _():
        tail_copy().wait_recv()

    incremental = local % 128 == 0

    def multiply(d, lhs_cols, rhs_rows, first):
        def tile(j, carry):
            cols = pl.ds(pl.multiple_of(j * wide, wide), wide)
            product = jnp.dot(
                tok[:, lhs_cols], held[d, rhs_rows, cols], preferred_element_type=F32
            )
            at = d * tiles + j
            if first:
                total[at] = product
            else:
                total[at] = total[at] + product
            return carry

        lax.fori_loop(0, tiles, tile, 0)

    def project_dt():
        def arrived(k, carry):
            dt_arrival(k)
            return carry

        lax.fori_loop(1, n, arrived, 0)
        together = block // local

        def add(j, sums):
            cols = pl.ds(pl.multiple_of(j * block, block), block)
            piece = held_dt[j * together]
            for m in range(1, together):
                piece = piece + held_dt[j * together + m]
            return sums + lax.dot_general(
                tok[0:length, cols], piece, LAST, preferred_element_type=F32
            )

        sums = lax.fori_loop(0, depth // block, add, jnp.zeros((length, HEADS), F32))
        dt_out[...] = sums.astype(BF16)

    def step(s, carry):
        @pl.when(s < n)
        def _():
            for t in range(streams):
                for d in range(2):
                    ring_arrival(d, t, s)

                    @pl.when(s < n - 1)
                    def _():
                        ring_copy(d, t, s + 1).start()

            for d in range(2):
                side_copy(d, s).start()

        @pl.when((s >= 2) & (s <= n))
        def _():
            for d in range(2):
                side_arrival(d, s - 1)
                core_copy(d, s - 1).start()

        @pl.when(s >= 3)
        def _():
            for d in range(2):
                core_arrival(d, s - 2)

        @pl.when(s == 1)
        def _():
            project_dt()

        if incremental:
            for d in range(2):
                owner = owner_of(d, s - 2)
                at = pl.ds(pl.multiple_of(owner * local, 128), local)

                @pl.when(s == 2)
                def _():
                    multiply(d, at, at, True)

                @pl.when(s > 2)
                def _():
                    multiply(d, at, at, False)

        return carry

    lax.fori_loop(1, n + 2, step, 0)
    if not incremental:
        for d in range(2):
            multiply(d, slice(0, 512), slice(0, 512), True)

            def more(j, carry):
                at = pl.ds(pl.multiple_of(j * 512, 512), 512)
                multiply(d, at, at, False)
                return carry

            lax.fori_loop(1, depth // 512, more, 0)

    for j in range(2 * tiles):
        cols = slice(j * wide, (j + 1) * wide)
        proj[:, cols] = total[j, 0:length].astype(BF16)
        tail[:, cols] = total[j, length:].astype(BF16)

    def drain(s, carry):
        for d in range(2):
            for t in range(streams):
                ring_copy(d, t, s).wait_send()
            side_copy(d, s).wait_send()
            core_copy(d, s).wait_send()
        dt_copy(s).wait_send()
        return carry

    lax.fori_loop(1, n, drain, 0)

    @pl.when(rank < ndev - 1)
    def _():
        tail_copy().wait_send()


def run_project(tokens, w_in, w_dt):
    n, n_out = lax.axis_size("inner"), lax.axis_size("outer")
    length, depth = tokens.shape
    local, xbc = w_in.shape
    block = max(local, 128)
    tail_rows = 16
    dt_block = w_dt.T
    if block != local:
        start = lax.rem(lax.axis_index("inner") * local, block)
        dt_block = lax.dynamic_update_slice(
            jnp.zeros((HEADS, block), BF16), dt_block, (jnp.int32(0), start)
        )
    streams = xbc // 4 // 128
    dma = pltpu.SemaphoreType.DMA
    vmem = pl.BlockSpec(memory_space=pltpu.VMEM)
    whole = pl.BlockSpec(memory_space=pl.ANY)
    return pl.pallas_call(
        partial(project_kernel, n, n_out),
        out_shape=(
            jax.ShapeDtypeStruct((length, xbc), BF16),
            jax.ShapeDtypeStruct((tail_rows, xbc), BF16),
            jax.ShapeDtypeStruct((length, HEADS), BF16),
        ),
        in_specs=[whole, whole, vmem],
        out_specs=(vmem, vmem, vmem),
        scratch_shapes=[
            pltpu.VMEM((length + tail_rows, depth), BF16),
            pltpu.VMEM((2, depth, xbc // 2), BF16),
            pltpu.VMEM((xbc // 256, length + tail_rows, 256), F32),
            pltpu.VMEM((n, HEADS, block), BF16),
            dma((2, streams, n)), dma((2, streams, n)),
            dma((2, n)), dma((2, n)), dma((2, n)), dma((2, n)),
            dma((n,)), dma((n,)), dma((3,)), dma(()), dma(()),
        ],
        compiler_params=pltpu.CompilerParams(
            collective_id=2, has_side_effects=True, vmem_limit_bytes=60 * 2**20
        ),
        name="project",
    )(tokens, w_in, dt_block)


def per_device(tokens, w_in, w_dt, conv_w, conv_b, dt_bias, a_log, d_skip, norm_gain):
    own_rows = tokens.reshape(tokens.shape[1], tokens.shape[2])
    row_count = own_rows.shape[0]
    projected, tail, dt_raw = run_project(own_rows, w_in, w_dt)
    mixed, entry = run_scan(
        projected, tail, dt_raw, conv_w, conv_b, dt_bias, a_log, d_skip, norm_gain
    )
    return (
        mixed.reshape(1, row_count, HP),
        entry.reshape(1, 1, HEADS, P_SIZE, N),
    )


def solution(mesh):
    placed = (
        P(("grp", "outer"), "inner", None),
        P("inner", None),
        P("inner", None),
        P(), P(), P(), P(), P(), P(),
    )
    return jax.shard_map(
        per_device,
        mesh=mesh,
        in_specs=placed,
        out_specs=(
            P(("grp", "outer"), "inner", None),
            P(("grp", "outer"), "inner", None, None, None),
        ),
        check_vma=False,
    )
```

```python
from functools import partial

import jax
import jax.numpy as jnp
from jax import lax
from jax.experimental import pallas as pl
from jax.experimental.pallas import tpu as pltpu
from jax.sharding import PartitionSpec as P

HEADS = 16
P_SIZE = 64
N = 256
CONV = 4
HP = HEADS * P_SIZE
CHUNK = 256
EPSILON = 1e-05
MESH = pl.DeviceIdType.MESH
F32 = jnp.float32
BF16 = jnp.bfloat16
LAST = (((1,), (1,)), ((), ()))
FIRST = (((0,), (0,)), ((), ()))


def expand(values, spread):
    high = values.astype(BF16)
    low = (values - high.astype(F32)).astype(BF16)
    return jnp.dot(high, spread, preferred_element_type=F32) + jnp.dot(
        low, spread, preferred_element_type=F32
    )


def scan_kernel(
    n_in, ndev,
    proj, tail, dt_raw, conv_w, conv_b, dt_bias, a_log, d_skip, gain,
    mixed, entry_out,
    bias_row, skip_row, pad, conv, log_s, log_t, step_s, y, states,
    send1, recv1, send2, recv2, dec_send, dec_recv,
    ss1, rs1, ss2, rs2, ssd, rsd,
):
    length = proj.shape[0]
    chunks = length // CHUNK
    rows = HP // ndev
    me = lax.axis_index("outer") * n_in + lax.axis_index("inner")

    def place(g):
        return {"inner": lax.rem(g, n_in), "outer": lax.div(g, n_in)}

    barrier = pltpu.get_barrier_semaphore()

    def greet(k, carry):
        pl.semaphore_signal(
            barrier, inc=1, device_id=place(lax.rem(me + k, ndev)), device_id_type=MESH
        )
        return carry

    lax.fori_loop(1, ndev, greet, 0)

    head_id = lax.broadcasted_iota(jnp.int32, (HEADS, HP), 0)
    col_head = lax.broadcasted_iota(jnp.int32, (HEADS, HP), 1) // P_SIZE
    spread = (head_id == col_head).astype(F32).astype(BF16)

    bias_row[...] = conv_b[...].reshape(1, conv_b.shape[0])
    gain_row = gain[...].reshape(1, HP)
    skip = d_skip[...].reshape(1, HEADS)
    skip_high = skip.astype(BF16).astype(F32)
    skip_row[...] = expand(skip - skip_high, spread) + jnp.dot(
        skip_high.astype(BF16), spread, preferred_element_type=F32
    )
    step_size = jax.nn.softplus(dt_raw[...].astype(F32) + dt_bias[...].reshape(1, HEADS))
    scaled = step_size * (-jnp.exp(a_log[...].reshape(1, HEADS)))
    row_id = lax.broadcasted_iota(jnp.int32, (CHUNK, CHUNK), 0)
    col_id = lax.broadcasted_iota(jnp.int32, (CHUNK, CHUNK), 1)
    causal = col_id <= row_id
    lower = causal.astype(F32)
    step_s[...] = step_size
    before = jnp.zeros((1, HEADS), F32)
    for c in range(chunks):
        part = jnp.dot(
            lower,
            scaled[c * CHUNK : (c + 1) * CHUNK],
            preferred_element_type=F32,
            precision=lax.Precision.HIGHEST,
        ) + before
        log_s[c * CHUNK : (c + 1) * CHUNK] = part
        before = part[CHUNK - 1 : CHUNK]
    log_t[...] = jnp.transpose(log_s[...])
    dec_send[...] = jnp.broadcast_to(jnp.exp(log_t[:, length - 1 : length]), (HEADS, 128))

    pad[0:8] = tail[...].astype(F32)[8:16]
    pad[8:] = proj[...].astype(F32)
    wide = 256
    blocks = proj.shape[1] // wide

    def conv_block(t, carry):
        i, j = lax.div(t, blocks), lax.rem(t, blocks)
        cols = pl.ds(pl.multiple_of(j * wide, wide), wide)
        window = pad[pl.ds(pl.multiple_of(i * 128, 128), 136), cols]
        total = bias_row[:, cols]
        for k in range(CONV):
            total = total + conv_w[k : k + 1, cols] * window[5 + k : 5 + k + 128]
        conv[pl.ds(pl.multiple_of(i * 128, 128), 128), cols] = (
            total * jax.nn.sigmoid(total)
        ).astype(BF16)
        return carry

    lax.fori_loop(0, (length // 128) * blocks, conv_block, 0)

    def weighted_sum(stop):
        final = log_s[stop - 1 : stop]
        factor = jnp.exp(final - log_s[0:stop]) * step_s[0:stop]
        weighted = (expand(factor, spread) * conv[0:stop, 0:HP].astype(F32)).astype(BF16)
        return lax.dot_general(
            weighted, conv[0:stop, HP : HP + N], FIRST, preferred_element_type=F32
        )

    send1[...] = weighted_sum(length).reshape(ndev, rows, N).astype(BF16)
    recv1[me] = send1[me]
    dec_recv[me] = dec_send[...]

    def decay_copy(g):
        return pltpu.make_async_remote_copy(
            src_ref=dec_send, dst_ref=dec_recv.at[me], send_sem=ssd.at[g],
            recv_sem=rsd.at[me], device_id=place(g), device_id_type=MESH,
        )

    def first_copy(g):
        return pltpu.make_async_remote_copy(
            src_ref=send1.at[g], dst_ref=recv1.at[me], send_sem=ss1.at[g],
            recv_sem=rs1.at[me], device_id=place(g), device_id_type=MESH,
        )

    def second_copy(g):
        return pltpu.make_async_remote_copy(
            src_ref=send2.at[g], dst_ref=recv2.at[me], send_sem=ss2.at[g],
            recv_sem=rs2.at[me], device_id=place(g), device_id_type=MESH,
        )

    pl.semaphore_wait(barrier, ndev - 1)

    def send_first(k, carry):
        g = lax.rem(me + k, ndev)
        decay_copy(g).start()
        first_copy(g).start()
        return carry

    lax.fori_loop(1, ndev, send_first, 0)

    states[0] = jnp.zeros((HP, N), BF16)
    for c in range(1, chunks):
        states[c] = weighted_sum(c * CHUNK).astype(BF16)

    def local_chunk(c, carry):
        start = pl.multiple_of(c * CHUNK, CHUNK)
        here = pl.ds(start, CHUNK)
        log_c = log_s[here]
        reached = log_s[pl.ds(pl.multiple_of(jnp.maximum(start - 8, 0), 8), 8)][7:8]
        reached = jnp.where(c > 0, reached, 0.0)
        c_rows = conv[here, HP + N :]
        b_rows = conv[here, HP : HP + N]
        scores = lax.dot_general(c_rows, b_rows, LAST, preferred_element_type=F32)
        scores = jnp.where(causal, scores, 0.0)
        x_rows = conv[here, 0:HP].astype(F32)
        driven = (expand(step_s[here], spread) * x_rows).astype(BF16)
        inter = lax.dot_general(c_rows, states[c], LAST, preferred_element_type=F32)
        y[here] = expand(jnp.exp(log_c - reached), spread) * inter + skip_row[...] * x_rows
        for h in range(0, HEADS, 2):
            pieces = []
            for k in (h, h + 1):
                gap = jnp.minimum(log_c[:, k : k + 1] - log_t[k : k + 1, here], 0.0)
                mixing = (scores * jnp.exp(gap)).astype(BF16)
                pieces.append(
                    jnp.dot(
                        mixing,
                        driven[:, k * P_SIZE : (k + 1) * P_SIZE],
                        preferred_element_type=F32,
                    )
                )
            both = slice(h * P_SIZE, (h + 2) * P_SIZE)
            y[here, both] = y[here, both] + jnp.concatenate(pieces, axis=1)
        return carry

    lax.fori_loop(0, chunks, local_chunk, 0)

    own_head = lax.div(me * rows, P_SIZE)

    def wait_from(copy_of, r):
        copy_of(r).wait_recv()

    def arrive(buffer, sems, r):
        pltpu.make_async_remote_copy(
            src_ref=buffer.at[r], dst_ref=buffer.at[r], send_sem=sems.at[r],
            recv_sem=sems.at[r], device_id=place(r), device_id_type=MESH,
        ).wait_recv()

    def advance(r, state):
        send2[r] = state.astype(BF16)

        @pl.when(r != me)
        def _():
            second_copy(r).start()
            arrive(dec_recv, rsd, r)
            arrive(recv1, rs1, r)

        decay = dec_recv[r, pl.ds(own_head, 1), :]
        decay = jnp.concatenate([decay, decay], axis=1)
        return decay * state + recv1[r].astype(F32)

    lax.fori_loop(0, ndev, advance, jnp.zeros((rows, N), F32))
    recv2[me] = send2[me]

    def finish(k, carry):
        g = lax.rem(me + k, ndev)
        arrive(recv2, rs2, g)
        decay_copy(g).wait_send()
        first_copy(g).wait_send()
        second_copy(g).wait_send()
        return carry

    lax.fori_loop(1, ndev, finish, 0)

    entry = recv2[...].astype(F32).reshape(HP, N)
    entry_out[...] = entry
    entry = entry.astype(BF16)
    for c in range(chunks):
        here = slice(c * CHUNK, (c + 1) * CHUNK)
        carried = lax.dot_general(
            conv[here, HP + N :], entry, LAST, preferred_element_type=F32
        )
        out = y[here] + expand(jnp.exp(log_s[here]), spread) * carried
        square = out * out
        high = square.astype(BF16)
        low = (square - high.astype(F32)).astype(BF16)
        sums = lax.dot_general(high, spread, LAST, preferred_element_type=F32)
        sums = sums + lax.dot_general(low, spread, LAST, preferred_element_type=F32)
        inv_rms = lax.rsqrt(sums * (1.0 / P_SIZE) + EPSILON)
        mixed[here] = (out * expand(inv_rms, spread) * gain_row).astype(BF16)


def run_scan(projected, tail, dt_raw, conv_w, conv_b, dt_bias, a_log, d_skip, norm_gain):
    n_in, n_out = lax.axis_size("inner"), lax.axis_size("outer")
    ndev = n_in * n_out
    length, xbc = projected.shape
    rows = HP // ndev
    dma = pltpu.SemaphoreType.DMA((ndev,))
    vmem = pl.BlockSpec(memory_space=pltpu.VMEM)
    return pl.pallas_call(
        partial(scan_kernel, n_in, ndev),
        out_shape=(
            jax.ShapeDtypeStruct((length, HP), BF16),
            jax.ShapeDtypeStruct((HP, N), F32),
        ),
        in_specs=[vmem] * 9,
        out_specs=(vmem, vmem),
        scratch_shapes=[
            pltpu.VMEM((1, xbc), F32),
            pltpu.VMEM((1, HP), F32),
            pltpu.VMEM((length + 8, xbc), F32),
            pltpu.VMEM((length, xbc), BF16),
            pltpu.VMEM((length, HEADS), F32),
            pltpu.VMEM((HEADS, length), F32),
            pltpu.VMEM((length, HEADS), F32),
            pltpu.VMEM((length, HP), F32),
            pltpu.VMEM((length // CHUNK, HP, N), BF16),
            pltpu.VMEM((ndev, rows, N), BF16),
            pltpu.VMEM((ndev, rows, N), BF16),
            pltpu.VMEM((ndev, rows, N), BF16),
            pltpu.VMEM((ndev, rows, N), BF16),
            pltpu.VMEM((HEADS, 128), F32),
            pltpu.VMEM((ndev, HEADS, 128), F32),
            dma, dma, dma, dma, dma, dma,
        ],
        compiler_params=pltpu.CompilerParams(
            collective_id=1, has_side_effects=True, vmem_limit_bytes=60 * 2**20
        ),
        name="scan",
    )(
        projected, tail, dt_raw, conv_w, conv_b, dt_bias, a_log, d_skip, norm_gain,
    )


def project_kernel(
    n, n_out,
    tokens, w_in, w_dt,
    proj, tail, dt_out,
    tok, held, total, held_dt,
    ring_s, ring_r, side_s, side_r, core_s, core_r, dt_s, dt_r, misc, tail_s, tail_r,
):
    length, depth = tokens.shape
    local, xbc = w_in.shape
    half = xbc // 2
    quarter = half // 2
    lanes = 128
    streams = quarter // lanes
    wide = 256
    tiles = half // wide
    third = (local * 5 // 16) // 16 * 16
    ring_rows = local - third
    tail_rows = tok.shape[0] - length
    block = held_dt.shape[2]
    ndev = n * n_out
    me = lax.axis_index("inner")
    core = lax.axis_index("outer")
    grp = lax.axis_index("grp")
    rank = core * n + me
    odd = lax.rem(me, 2)
    pos = jnp.where(odd == 0, lax.div(me, 2), n - lax.div(me + 1, 2))

    def index_at(q):
        q = lax.rem(q + 2 * n, n)
        return jnp.where(q < n // 2, 2 * q, 2 * n - 1 - 2 * q)

    def place(g):
        return {"inner": lax.rem(g, n), "outer": lax.div(g, n)}

    barrier = pltpu.get_barrier_semaphore()

    def greet(k, carry):
        pl.semaphore_signal(
            barrier, inc=1, device_id=place(lax.rem(rank + k, ndev)), device_id_type=MESH
        )
        return carry

    lax.fori_loop(1, ndev, greet, 0)
    pl.semaphore_signal(barrier, inc=1, device_id={"grp": 1 - grp}, device_id_type=MESH)

    def own_rows(owner):
        return pl.ds(pl.multiple_of(owner * local, 16), local)

    load_tok = pltpu.make_async_copy(tokens, tok.at[pl.ds(0, length)], misc.at[0])
    load_w = [
        pltpu.make_async_copy(
            w_in.at[:, pl.ds(d * half, half)], held.at[d, own_rows(me)], misc.at[1 + d]
        )
        for d in range(2)
    ]
    for copy in load_w:
        copy.start()
    load_tok.start()
    held_dt[me] = w_dt[...]

    @pl.when(rank == 0)
    def _():
        tok[length:] = jnp.zeros((tail_rows, depth), BF16)

    def ring_copy(d, t, s):
        owner = index_at(pos - (s - 1)) if d == 0 else index_at(pos + (s - 1))
        target = index_at(pos + 1) if d == 0 else index_at(pos - 1)
        rows = pl.ds(pl.multiple_of(owner * local + grp * third, 16), ring_rows)
        cols = pl.ds(pl.multiple_of(core * quarter + t * lanes, lanes), lanes)
        part = held.at[d, rows, cols]
        return pltpu.make_async_remote_copy(
            src_ref=part, dst_ref=part, send_sem=ring_s.at[d, t, s],
            recv_sem=ring_r.at[d, t, s], device_id={"inner": target}, device_id_type=MESH,
        )

    def owner_of(d, s):
        return index_at(pos - s) if d == 0 else index_at(pos + s)

    def chunk_cols(which, t):
        return pl.ds(pl.multiple_of(which * quarter + t * lanes, lanes), lanes)

    def side_rows(d, s, which):
        start = owner_of(d, s) * local + which * ring_rows
        return pl.ds(pl.multiple_of(start, 16), third)

    def side_between(d, t, s, which):
        part = held.at[d, side_rows(d, s, which), chunk_cols(core, t)]
        return pltpu.make_async_remote_copy(
            src_ref=part, dst_ref=part, send_sem=side_s.at[d, t, s],
            recv_sem=side_r.at[d, t, s], device_id={"grp": 1 - grp}, device_id_type=MESH,
        )

    def core_between(d, t, s, which):
        part = held.at[d, own_rows(owner_of(d, s)), chunk_cols(which, t)]
        return pltpu.make_async_remote_copy(
            src_ref=part, dst_ref=part, send_sem=core_s.at[d, t, s],
            recv_sem=core_r.at[d, t, s], device_id={"outer": 1 - core}, device_id_type=MESH,
        )

    def side_copy(d, t, s):
        return side_between(d, t, s, grp)

    def core_copy(d, t, s):
        return core_between(d, t, s, core)

    def ring_arrival(d, t, s):
        start = owner_of(d, s) * local + grp * third
        rows = pl.ds(pl.multiple_of(start, 16), ring_rows)
        part = held.at[d, rows, chunk_cols(core, t)]
        pltpu.make_async_remote_copy(
            src_ref=part, dst_ref=part, send_sem=ring_s.at[d, t, s],
            recv_sem=ring_r.at[d, t, s], device_id={"inner": index_at(pos + 1)},
            device_id_type=MESH,
        ).wait_recv()

    def side_arrival(d, t, s):
        side_between(d, t, s, 1 - grp).wait_recv()

    def core_arrival(d, t, s):
        core_between(d, t, s, 1 - core).wait_recv()

    def dt_copy(k):
        peer = lax.rem(me + k, n)
        return pltpu.make_async_remote_copy(
            src_ref=w_dt, dst_ref=held_dt.at[me], send_sem=dt_s.at[k],
            recv_sem=dt_r.at[me], device_id={"inner": peer}, device_id_type=MESH,
        )

    def dt_arrival(k):
        peer = lax.rem(me + k, n)
        pltpu.make_async_remote_copy(
            src_ref=w_dt, dst_ref=held_dt.at[peer], send_sem=dt_s.at[k],
            recv_sem=dt_r.at[peer], device_id={"inner": peer}, device_id_type=MESH,
        ).wait_recv()

    def tail_copy():
        return pltpu.make_async_remote_copy(
            src_ref=tokens.at[pl.ds(length - tail_rows, tail_rows)],
            dst_ref=tok.at[pl.ds(length, tail_rows)], send_sem=tail_s,
            recv_sem=tail_r, device_id=place(lax.rem(rank + 1, ndev)), device_id_type=MESH,
        )

    pl.semaphore_wait(barrier, ndev)

    @pl.when(rank < ndev - 1)
    def _():
        tail_copy().start()

    for d in range(2):
        load_w[d].wait()
        for t in range(streams):
            ring_copy(d, t, 1).start()

    def send_dt(k, carry):
        dt_copy(k).start()
        return carry

    lax.fori_loop(1, n, send_dt, 0)
    load_tok.wait()

    @pl.when(rank > 0)
    def _():
        tail_copy().wait_recv()

    incremental = local % 128 == 0

    def multiply_tile(d, lhs_cols, rhs_rows, first, j):
        cols = pl.ds(pl.multiple_of(j * wide, wide), wide)
        product = jnp.dot(
            tok[:, lhs_cols], held[d, rhs_rows, cols], preferred_element_type=F32
        )
        at = d * tiles + j
        if first:
            total[at] = product
        else:
            total[at] = total[at] + product

    def multiply(d, lhs_cols, rhs_rows, first):
        def tile(j, carry):
            multiply_tile(d, lhs_cols, rhs_rows, first, j)
            return carry

        lax.fori_loop(0, tiles, tile, 0)

    def project_dt():
        def arrived(k, carry):
            dt_arrival(k)
            return carry

        lax.fori_loop(1, n, arrived, 0)
        together = block // local

        def add(j, sums):
            cols = pl.ds(pl.multiple_of(j * block, block), block)
            piece = held_dt[j * together]
            for m in range(1, together):
                piece = piece + held_dt[j * together + m]
            return sums + lax.dot_general(
                tok[0:length, cols], piece, LAST, preferred_element_type=F32
            )

        sums = lax.fori_loop(0, depth // block, add, jnp.zeros((length, HEADS), F32))
        dt_out[...] = sums.astype(BF16)

    def step(s, carry):
        @pl.when(s >= 3)
        def _():
            for t in range(streams):
                for d in range(2):
                    core_arrival(d, t, s - 2)

        def part(t, inner):
            @pl.when(s < n)
            def _():
                for d in range(2):
                    ring_arrival(d, t, s)

                    @pl.when(s < n - 1)
                    def _():
                        ring_copy(d, t, s + 1).start()

                    side_copy(d, t, s).start()

            @pl.when((s >= 2) & (s <= n))
            def _():
                for d in range(2):
                    side_arrival(d, t, s - 1)
                    core_copy(d, t, s - 1).start()

            if incremental:
                for d in range(2):
                    owner = owner_of(d, s - 2)
                    at = pl.ds(pl.multiple_of(owner * local, 128), local)

                    @pl.when(s == 2)
                    def _():
                        multiply_tile(d, at, at, True, t)

                    @pl.when(s > 2)
                    def _():
                        multiply_tile(d, at, at, False, t)

            return inner

        lax.fori_loop(0, streams, part, 0)

        @pl.when(s == 1)
        def _():
            project_dt()

        return carry

    lax.fori_loop(1, n + 2, step, 0)
    if not incremental:
        for d in range(2):
            multiply(d, slice(0, 512), slice(0, 512), True)

            def more(j, carry):
                at = pl.ds(pl.multiple_of(j * 512, 512), 512)
                multiply(d, at, at, False)
                return carry

            lax.fori_loop(1, depth // 512, more, 0)

    for j in range(2 * tiles):
        cols = slice(j * wide, (j + 1) * wide)
        proj[:, cols] = total[j, 0:length].astype(BF16)
        tail[:, cols] = total[j, length:].astype(BF16)

    def drain(s, carry):
        for d in range(2):
            for t in range(streams):
                ring_copy(d, t, s).wait_send()
                side_copy(d, t, s).wait_send()
                core_copy(d, t, s).wait_send()
        dt_copy(s).wait_send()
        return carry

    lax.fori_loop(1, n, drain, 0)

    @pl.when(rank < ndev - 1)
    def _():
        tail_copy().wait_send()


def run_project(tokens, w_in, w_dt):
    n, n_out = lax.axis_size("inner"), lax.axis_size("outer")
    length, depth = tokens.shape
    local, xbc = w_in.shape
    block = max(local, 128)
    tail_rows = 16
    dt_block = w_dt.T
    if block != local:
        start = lax.rem(lax.axis_index("inner") * local, block)
        dt_block = lax.dynamic_update_slice(
            jnp.zeros((HEADS, block), BF16), dt_block, (jnp.int32(0), start)
        )
    streams = xbc // 4 // 128
    dma = pltpu.SemaphoreType.DMA
    vmem = pl.BlockSpec(memory_space=pltpu.VMEM)
    whole = pl.BlockSpec(memory_space=pl.ANY)
    return pl.pallas_call(
        partial(project_kernel, n, n_out),
        out_shape=(
            jax.ShapeDtypeStruct((length, xbc), BF16),
            jax.ShapeDtypeStruct((tail_rows, xbc), BF16),
            jax.ShapeDtypeStruct((length, HEADS), BF16),
        ),
        in_specs=[whole, whole, vmem],
        out_specs=(vmem, vmem, vmem),
        scratch_shapes=[
            pltpu.VMEM((length + tail_rows, depth), BF16),
            pltpu.VMEM((2, depth, xbc // 2), BF16),
            pltpu.VMEM((xbc // 256, length + tail_rows, 256), F32),
            pltpu.VMEM((n, HEADS, block), BF16),
            dma((2, streams, n)), dma((2, streams, n)),
            dma((2, streams, n)), dma((2, streams, n)),
            dma((2, streams, n)), dma((2, streams, n)),
            dma((n,)), dma((n,)), dma((3,)), dma(()), dma(()),
        ],
        compiler_params=pltpu.CompilerParams(
            collective_id=2, has_side_effects=True, vmem_limit_bytes=60 * 2**20
        ),
        name="project",
    )(tokens, w_in, dt_block)


def per_device(tokens, w_in, w_dt, conv_w, conv_b, dt_bias, a_log, d_skip, norm_gain):
    own_rows = tokens.reshape(tokens.shape[1], tokens.shape[2])
    row_count = own_rows.shape[0]
    projected, tail, dt_raw = run_project(own_rows, w_in, w_dt)
    mixed, entry = run_scan(
        projected, tail, dt_raw, conv_w, conv_b, dt_bias, a_log, d_skip, norm_gain
    )
    return (
        mixed.reshape(1, row_count, HP),
        entry.reshape(1, 1, HEADS, P_SIZE, N),
    )


def solution(mesh):
    placed = (
        P(("grp", "outer"), "inner", None),
        P("inner", None),
        P("inner", None),
        P(), P(), P(), P(), P(), P(),
    )
    return jax.shard_map(
        per_device,
        mesh=mesh,
        in_specs=placed,
        out_specs=(
            P(("grp", "outer"), "inner", None),
            P(("grp", "outer"), "inner", None, None, None),
        ),
        check_vma=False,
    )
```

```python
from functools import partial

import jax
import jax.numpy as jnp
from jax import lax
from jax.experimental import pallas as pl
from jax.experimental.pallas import tpu as pltpu
from jax.sharding import PartitionSpec as P

HEADS = 16
P_SIZE = 64
N = 256
CONV = 4
HP = HEADS * P_SIZE
CHUNK = 256
EPSILON = 1e-05
MESH = pl.DeviceIdType.MESH
F32 = jnp.float32
BF16 = jnp.bfloat16
LAST = (((1,), (1,)), ((), ()))
FIRST = (((0,), (0,)), ((), ()))


def expand(values, spread):
    high = values.astype(BF16)
    low = (values - high.astype(F32)).astype(BF16)
    return jnp.dot(high, spread, preferred_element_type=F32) + jnp.dot(
        low, spread, preferred_element_type=F32
    )


def scan_kernel(
    n_in, ndev,
    proj, tail, dt_raw, conv_w, conv_b, dt_bias, a_log, d_skip, gain,
    mixed, entry_out,
    gain_s, bias_row, skip_row, pad, conv, log_s, log_t, step_s, y, states,
    send1, recv1, send2, recv2, dec_send, dec_recv,
    ss1, rs1, ss2, rs2, ssd, rsd,
):
    length = proj.shape[0]
    chunks = length // CHUNK
    rows = HP // ndev
    me = lax.axis_index("outer") * n_in + lax.axis_index("inner")

    def place(g):
        return {"inner": lax.rem(g, n_in), "outer": lax.div(g, n_in)}

    barrier = pltpu.get_barrier_semaphore()

    def greet(k, carry):
        pl.semaphore_signal(
            barrier, inc=1, device_id=place(lax.rem(me + k, ndev)), device_id_type=MESH
        )
        return carry

    lax.fori_loop(1, ndev, greet, 0)

    head_id = lax.broadcasted_iota(jnp.int32, (HEADS, HP), 0)
    col_head = lax.broadcasted_iota(jnp.int32, (HEADS, HP), 1) // P_SIZE
    spread = (head_id == col_head).astype(F32).astype(BF16)

    bias_row[...] = conv_b[...].reshape(1, conv_b.shape[0])
    gain_s[...] = gain[...].reshape(1, HP)
    skip = d_skip[...].reshape(1, HEADS)
    skip_high = skip.astype(BF16).astype(F32)
    skip_row[...] = expand(skip - skip_high, spread) + jnp.dot(
        skip_high.astype(BF16), spread, preferred_element_type=F32
    )
    step_size = jax.nn.softplus(dt_raw[...].astype(F32) + dt_bias[...].reshape(1, HEADS))
    scaled = step_size * (-jnp.exp(a_log[...].reshape(1, HEADS)))
    row_id = lax.broadcasted_iota(jnp.int32, (CHUNK, CHUNK), 0)
    col_id = lax.broadcasted_iota(jnp.int32, (CHUNK, CHUNK), 1)
    causal = col_id <= row_id
    lower = causal.astype(F32)
    step_s[...] = step_size
    before = jnp.zeros((1, HEADS), F32)
    for c in range(chunks):
        part = jnp.dot(
            lower,
            scaled[c * CHUNK : (c + 1) * CHUNK],
            preferred_element_type=F32,
            precision=lax.Precision.HIGHEST,
        ) + before
        log_s[c * CHUNK : (c + 1) * CHUNK] = part
        before = part[CHUNK - 1 : CHUNK]
    log_t[...] = jnp.transpose(log_s[...])
    dec_send[...] = jnp.broadcast_to(jnp.exp(log_t[:, length - 1 : length]), (HEADS, 128))

    pad[0:8] = tail[...].astype(F32)[8:16]
    pad[8:] = proj[...].astype(F32)
    wide = 256
    blocks = proj.shape[1] // wide

    def conv_block(t, carry):
        i, j = lax.div(t, blocks), lax.rem(t, blocks)
        cols = pl.ds(pl.multiple_of(j * wide, wide), wide)
        window = pad[pl.ds(pl.multiple_of(i * 128, 128), 136), cols]
        total = bias_row[:, cols]
        for k in range(CONV):
            total = total + conv_w[k : k + 1, cols] * window[5 + k : 5 + k + 128]
        conv[pl.ds(pl.multiple_of(i * 128, 128), 128), cols] = (
            total * jax.nn.sigmoid(total)
        ).astype(BF16)
        return carry

    row_blocks = length // 128

    def conv_column(j):
        def one(i, carry):
            return conv_block(i * blocks + j, carry)

        lax.fori_loop(0, row_blocks, one, 0)

    conv_column(HP // wide)

    def weighted_sum(stop):
        final = log_s[stop - 1 : stop]
        factor = jnp.exp(final - log_s[0:stop]) * step_s[0:stop]
        weighted = (expand(factor, spread) * conv[0:stop, 0:HP].astype(F32)).astype(BF16)
        return lax.dot_general(
            weighted, conv[0:stop, HP : HP + N], FIRST, preferred_element_type=F32
        )

    dec_recv[me] = dec_send[...]

    def decay_copy(g):
        return pltpu.make_async_remote_copy(
            src_ref=dec_send, dst_ref=dec_recv.at[me], send_sem=ssd.at[g],
            recv_sem=rsd.at[me], device_id=place(g), device_id_type=MESH,
        )

    def first_copy(g):
        return pltpu.make_async_remote_copy(
            src_ref=send1.at[g], dst_ref=recv1.at[me], send_sem=ss1.at[g],
            recv_sem=rs1.at[me], device_id=place(g), device_id_type=MESH,
        )

    def second_copy(g):
        return pltpu.make_async_remote_copy(
            src_ref=send2.at[g], dst_ref=recv2.at[me], send_sem=ss2.at[g],
            recv_sem=rs2.at[me], device_id=place(g), device_id_type=MESH,
        )

    pl.semaphore_wait(barrier, ndev - 1)

    def send_decay(k, carry):
        decay_copy(lax.rem(me + k, ndev)).start()
        return carry

    lax.fori_loop(1, ndev, send_decay, 0)

    groups = HP // wide
    owners = ndev // groups
    own_group = lax.div(me, owners)
    factor = jnp.exp(log_s[length - 1 : length] - log_s[...]) * step_s[...]

    def spread_of(j):
        head = lax.broadcasted_iota(jnp.int32, (HEADS, wide), 0)
        col = lax.broadcasted_iota(jnp.int32, (HEADS, wide), 1) // P_SIZE
        return (head == col + j * (wide // P_SIZE)).astype(F32).astype(BF16)

    def first_group(i, carry):
        j = lax.rem(own_group + 1 + i, groups)
        conv_column(j)
        cols = pl.ds(pl.multiple_of(j * wide, wide), wide)
        weighted = (expand(factor, spread_of(j)) * conv[:, cols].astype(F32)).astype(BF16)
        part = lax.dot_general(
            weighted, conv[:, HP : HP + N], FIRST, preferred_element_type=F32
        )
        send1[pl.ds(j * owners, owners)] = part.reshape(owners, rows, N).astype(BF16)

        def send_one(k, inner):
            g = j * owners + k

            @pl.when(g != me)
            def _():
                first_copy(g).start()

            return inner

        return lax.fori_loop(0, owners, send_one, carry)

    lax.fori_loop(0, groups, first_group, 0)
    recv1[me] = send1[me]
    conv_column(HP // wide + 1)

    states[0] = jnp.zeros((HP, N), BF16)
    for c in range(1, chunks):
        states[c] = weighted_sum(c * CHUNK).astype(BF16)

    def local_chunk(c, carry):
        start = pl.multiple_of(c * CHUNK, CHUNK)
        here = pl.ds(start, CHUNK)
        log_c = log_s[here]
        reached = log_s[pl.ds(pl.multiple_of(jnp.maximum(start - 8, 0), 8), 8)][7:8]
        reached = jnp.where(c > 0, reached, 0.0)
        c_rows = conv[here, HP + N :]
        b_rows = conv[here, HP : HP + N]
        scores = lax.dot_general(c_rows, b_rows, LAST, preferred_element_type=F32)
        scores = jnp.where(causal, scores, 0.0)
        x_rows = conv[here, 0:HP].astype(F32)
        driven = (expand(step_s[here], spread) * x_rows).astype(BF16)
        inter = lax.dot_general(c_rows, states[c], LAST, preferred_element_type=F32)
        y[here] = expand(jnp.exp(log_c - reached), spread) * inter + skip_row[...] * x_rows
        for h in range(0, HEADS, 2):
            pieces = []
            for k in (h, h + 1):
                gap = jnp.minimum(log_c[:, k : k + 1] - log_t[k : k + 1, here], 0.0)
                mixing = (scores * jnp.exp(gap)).astype(BF16)
                pieces.append(
                    jnp.dot(
                        mixing,
                        driven[:, k * P_SIZE : (k + 1) * P_SIZE],
                        preferred_element_type=F32,
                    )
                )
            both = slice(h * P_SIZE, (h + 2) * P_SIZE)
            y[here, both] = y[here, both] + jnp.concatenate(pieces, axis=1)
        return carry

    lax.fori_loop(0, chunks, local_chunk, 0)

    own_head = lax.div(me * rows, P_SIZE)

    def wait_from(copy_of, r):
        copy_of(r).wait_recv()

    def arrive(buffer, sems, r):
        pltpu.make_async_remote_copy(
            src_ref=buffer.at[r], dst_ref=buffer.at[r], send_sem=sems.at[r],
            recv_sem=sems.at[r], device_id=place(r), device_id_type=MESH,
        ).wait_recv()

    def advance(r, state):
        send2[r] = state.astype(BF16)

        @pl.when(r != me)
        def _():
            arrive(dec_recv, rsd, r)
            arrive(recv1, rs1, r)

        decay = dec_recv[r, pl.ds(own_head, 1), :]
        decay = jnp.concatenate([decay, decay], axis=1)
        return decay * state + recv1[r].astype(F32)

    lax.fori_loop(0, ndev, advance, jnp.zeros((rows, N), F32))

    def send_second(k, carry):
        second_copy(lax.rem(me + k, ndev)).start()
        return carry

    lax.fori_loop(1, ndev, send_second, 0)
    recv2[me] = send2[me]

    reach = jnp.exp(log_s[...])

    def last_group(i, carry):
        j = lax.rem(own_group + groups - 1 - i, groups)

        def wait_one(k, inner):
            g = j * owners + k

            @pl.when(g != me)
            def _():
                arrive(recv2, rs2, g)

            return inner

        lax.fori_loop(0, owners, wait_one, 0)
        cols = pl.ds(pl.multiple_of(j * wide, wide), wide)
        entry = recv2[pl.ds(j * owners, owners)].astype(F32).reshape(wide, N)
        entry_out[cols] = entry
        carried = lax.dot_general(
            conv[:, HP + N :], entry.astype(BF16), LAST, preferred_element_type=F32
        )
        spread_j = spread_of(j)
        out = y[:, cols] + expand(reach, spread_j) * carried
        square = out * out
        high = square.astype(BF16)
        low = (square - high.astype(F32)).astype(BF16)
        sums = lax.dot_general(high, spread_j, LAST, preferred_element_type=F32)
        sums = sums + lax.dot_general(low, spread_j, LAST, preferred_element_type=F32)
        inv_rms = lax.rsqrt(sums * (1.0 / P_SIZE) + EPSILON)
        mixed[:, cols] = (out * expand(inv_rms, spread_j) * gain_s[:, cols]).astype(BF16)
        return carry

    lax.fori_loop(0, groups, last_group, 0)

    def finish(k, carry):
        g = lax.rem(me + k, ndev)
        decay_copy(g).wait_send()
        first_copy(g).wait_send()
        second_copy(g).wait_send()
        return carry

    lax.fori_loop(1, ndev, finish, 0)


def run_scan(projected, tail, dt_raw, conv_w, conv_b, dt_bias, a_log, d_skip, norm_gain):
    n_in, n_out = lax.axis_size("inner"), lax.axis_size("outer")
    ndev = n_in * n_out
    length, xbc = projected.shape
    rows = HP // ndev
    dma = pltpu.SemaphoreType.DMA((ndev,))
    vmem = pl.BlockSpec(memory_space=pltpu.VMEM)
    return pl.pallas_call(
        partial(scan_kernel, n_in, ndev),
        out_shape=(
            jax.ShapeDtypeStruct((length, HP), BF16),
            jax.ShapeDtypeStruct((HP, N), F32),
        ),
        in_specs=[vmem] * 9,
        out_specs=(vmem, vmem),
        scratch_shapes=[
            pltpu.VMEM((1, HP), F32),
            pltpu.VMEM((1, xbc), F32),
            pltpu.VMEM((1, HP), F32),
            pltpu.VMEM((length + 8, xbc), F32),
            pltpu.VMEM((length, xbc), BF16),
            pltpu.VMEM((length, HEADS), F32),
            pltpu.VMEM((HEADS, length), F32),
            pltpu.VMEM((length, HEADS), F32),
            pltpu.VMEM((length, HP), F32),
            pltpu.VMEM((length // CHUNK, HP, N), BF16),
            pltpu.VMEM((ndev, rows, N), BF16),
            pltpu.VMEM((ndev, rows, N), BF16),
            pltpu.VMEM((ndev, rows, N), BF16),
            pltpu.VMEM((ndev, rows, N), BF16),
            pltpu.VMEM((HEADS, 128), F32),
            pltpu.VMEM((ndev, HEADS, 128), F32),
            dma, dma, dma, dma, dma, dma,
        ],
        compiler_params=pltpu.CompilerParams(
            collective_id=1, has_side_effects=True, vmem_limit_bytes=60 * 2**20
        ),
        name="scan",
    )(
        projected, tail, dt_raw, conv_w, conv_b, dt_bias, a_log, d_skip, norm_gain,
    )


def project_kernel(
    n, n_out,
    tokens, w_in, w_dt,
    proj, tail, dt_out,
    tok, held, total, held_dt,
    ring_s, ring_r, side_s, side_r, core_s, core_r, dt_s, dt_r, misc, tail_s, tail_r,
):
    length, depth = tokens.shape
    local, xbc = w_in.shape
    half = xbc // 2
    quarter = half // 2
    lanes = 128
    streams = quarter // lanes
    wide = 256
    tiles = half // wide
    third = (local * 5 // 16) // 16 * 16
    ring_rows = local - third
    tail_rows = tok.shape[0] - length
    block = held_dt.shape[2]
    ndev = n * n_out
    me = lax.axis_index("inner")
    core = lax.axis_index("outer")
    grp = lax.axis_index("grp")
    rank = core * n + me
    odd = lax.rem(me, 2)
    pos = jnp.where(odd == 0, lax.div(me, 2), n - lax.div(me + 1, 2))

    def index_at(q):
        q = lax.rem(q + 2 * n, n)
        return jnp.where(q < n // 2, 2 * q, 2 * n - 1 - 2 * q)

    def place(g):
        return {"inner": lax.rem(g, n), "outer": lax.div(g, n)}

    barrier = pltpu.get_barrier_semaphore()

    def greet(k, carry):
        pl.semaphore_signal(
            barrier, inc=1, device_id=place(lax.rem(rank + k, ndev)), device_id_type=MESH
        )
        return carry

    lax.fori_loop(1, ndev, greet, 0)
    pl.semaphore_signal(barrier, inc=1, device_id={"grp": 1 - grp}, device_id_type=MESH)

    def own_rows(owner):
        return pl.ds(pl.multiple_of(owner * local, 16), local)

    load_tok = pltpu.make_async_copy(tokens, tok.at[pl.ds(0, length)], misc.at[0])
    load_w = [
        pltpu.make_async_copy(
            w_in.at[:, pl.ds(d * half, half)], held.at[d, own_rows(me)], misc.at[1 + d]
        )
        for d in range(2)
    ]
    for copy in load_w:
        copy.start()
    load_tok.start()
    held_dt[me] = w_dt[...]

    @pl.when(rank == 0)
    def _():
        tok[length:] = jnp.zeros((tail_rows, depth), BF16)

    def ring_copy(d, t, s):
        owner = index_at(pos - (s - 1)) if d == 0 else index_at(pos + (s - 1))
        target = index_at(pos + 1) if d == 0 else index_at(pos - 1)
        rows = pl.ds(pl.multiple_of(owner * local + grp * third, 16), ring_rows)
        cols = pl.ds(pl.multiple_of(core * quarter + t * lanes, lanes), lanes)
        part = held.at[d, rows, cols]
        return pltpu.make_async_remote_copy(
            src_ref=part, dst_ref=part, send_sem=ring_s.at[d, t, s],
            recv_sem=ring_r.at[d, t, s], device_id={"inner": target}, device_id_type=MESH,
        )

    def owner_of(d, s):
        return index_at(pos - s) if d == 0 else index_at(pos + s)

    def chunk_cols(which, t):
        return pl.ds(pl.multiple_of(which * quarter + t * lanes, lanes), lanes)

    def side_rows(d, s, which):
        start = owner_of(d, s) * local + which * ring_rows
        return pl.ds(pl.multiple_of(start, 16), third)

    def side_between(d, t, s, which):
        part = held.at[d, side_rows(d, s, which), chunk_cols(core, t)]
        return pltpu.make_async_remote_copy(
            src_ref=part, dst_ref=part, send_sem=side_s.at[d, t, s],
            recv_sem=side_r.at[d, t, s], device_id={"grp": 1 - grp}, device_id_type=MESH,
        )

    def core_between(d, t, s, which):
        part = held.at[d, own_rows(owner_of(d, s)), chunk_cols(which, t)]
        return pltpu.make_async_remote_copy(
            src_ref=part, dst_ref=part, send_sem=core_s.at[d, t, s],
            recv_sem=core_r.at[d, t, s], device_id={"outer": 1 - core}, device_id_type=MESH,
        )

    def side_copy(d, t, s):
        return side_between(d, t, s, grp)

    def core_copy(d, t, s):
        return core_between(d, t, s, core)

    def ring_arrival(d, t, s):
        start = owner_of(d, s) * local + grp * third
        rows = pl.ds(pl.multiple_of(start, 16), ring_rows)
        part = held.at[d, rows, chunk_cols(core, t)]
        pltpu.make_async_remote_copy(
            src_ref=part, dst_ref=part, send_sem=ring_s.at[d, t, s],
            recv_sem=ring_r.at[d, t, s], device_id={"inner": index_at(pos + 1)},
            device_id_type=MESH,
        ).wait_recv()

    def side_arrival(d, t, s):
        side_between(d, t, s, 1 - grp).wait_recv()

    def core_arrival(d, t, s):
        core_between(d, t, s, 1 - core).wait_recv()

    def dt_copy(k):
        peer = lax.rem(me + k, n)
        return pltpu.make_async_remote_copy(
            src_ref=w_dt, dst_ref=held_dt.at[me], send_sem=dt_s.at[k],
            recv_sem=dt_r.at[me], device_id={"inner": peer}, device_id_type=MESH,
        )

    def dt_arrival(k):
        peer = lax.rem(me + k, n)
        pltpu.make_async_remote_copy(
            src_ref=w_dt, dst_ref=held_dt.at[peer], send_sem=dt_s.at[k],
            recv_sem=dt_r.at[peer], device_id={"inner": peer}, device_id_type=MESH,
        ).wait_recv()

    def tail_copy():
        return pltpu.make_async_remote_copy(
            src_ref=tokens.at[pl.ds(length - tail_rows, tail_rows)],
            dst_ref=tok.at[pl.ds(length, tail_rows)], send_sem=tail_s,
            recv_sem=tail_r, device_id=place(lax.rem(rank + 1, ndev)), device_id_type=MESH,
        )

    pl.semaphore_wait(barrier, ndev)

    @pl.when(rank < ndev - 1)
    def _():
        tail_copy().start()

    for d in range(2):
        load_w[d].wait()
        for t in range(streams):
            ring_copy(d, t, 1).start()

    def send_dt(k, carry):
        dt_copy(k).start()
        return carry

    lax.fori_loop(1, n, send_dt, 0)
    load_tok.wait()

    @pl.when(rank > 0)
    def _():
        tail_copy().wait_recv()

    incremental = local % 128 == 0

    def multiply_tile(d, lhs_cols, rhs_rows, first, j):
        cols = pl.ds(pl.multiple_of(j * wide, wide), wide)
        product = jnp.dot(
            tok[:, lhs_cols], held[d, rhs_rows, cols], preferred_element_type=F32
        )
        at = d * tiles + j
        if first:
            total[at] = product
        else:
            total[at] = total[at] + product

    def multiply(d, lhs_cols, rhs_rows, first):
        def tile(j, carry):
            multiply_tile(d, lhs_cols, rhs_rows, first, j)
            return carry

        lax.fori_loop(0, tiles, tile, 0)

    def project_dt():
        def arrived(k, carry):
            dt_arrival(k)
            return carry

        lax.fori_loop(1, n, arrived, 0)
        together = block // local

        def add(j, sums):
            cols = pl.ds(pl.multiple_of(j * block, block), block)
            piece = held_dt[j * together]
            for m in range(1, together):
                piece = piece + held_dt[j * together + m]
            return sums + lax.dot_general(
                tok[0:length, cols], piece, LAST, preferred_element_type=F32
            )

        sums = lax.fori_loop(0, depth // block, add, jnp.zeros((length, HEADS), F32))
        dt_out[...] = sums.astype(BF16)

    def step(s, carry):
        @pl.when(s >= 3)
        def _():
            for t in range(streams):
                for d in range(2):
                    core_arrival(d, t, s - 2)

        def part(t, inner):
            @pl.when(s < n)
            def _():
                for d in range(2):
                    ring_arrival(d, t, s)

                    @pl.when(s < n - 1)
                    def _():
                        ring_copy(d, t, s + 1).start()

                    side_copy(d, t, s).start()

            @pl.when((s >= 2) & (s <= n))
            def _():
                for d in range(2):
                    side_arrival(d, t, s - 1)
                    core_copy(d, t, s - 1).start()

            if incremental:
                for d in range(2):
                    owner = owner_of(d, s - 2)
                    at = pl.ds(pl.multiple_of(owner * local, 128), local)

                    @pl.when(s == 2)
                    def _():
                        multiply_tile(d, at, at, True, t)

                    @pl.when(s > 2)
                    def _():
                        multiply_tile(d, at, at, False, t)

            return inner

        lax.fori_loop(0, streams, part, 0)

        @pl.when(s == 1)
        def _():
            project_dt()

        return carry

    lax.fori_loop(1, n + 2, step, 0)
    if not incremental:
        for d in range(2):
            multiply(d, slice(0, 512), slice(0, 512), True)

            def more(j, carry):
                at = pl.ds(pl.multiple_of(j * 512, 512), 512)
                multiply(d, at, at, False)
                return carry

            lax.fori_loop(1, depth // 512, more, 0)

    for j in range(2 * tiles):
        cols = slice(j * wide, (j + 1) * wide)
        proj[:, cols] = total[j, 0:length].astype(BF16)
        tail[:, cols] = total[j, length:].astype(BF16)

    def drain(s, carry):
        for d in range(2):
            for t in range(streams):
                ring_copy(d, t, s).wait_send()
                side_copy(d, t, s).wait_send()
                core_copy(d, t, s).wait_send()
        dt_copy(s).wait_send()
        return carry

    lax.fori_loop(1, n, drain, 0)

    @pl.when(rank < ndev - 1)
    def _():
        tail_copy().wait_send()


def run_project(tokens, w_in, w_dt):
    n, n_out = lax.axis_size("inner"), lax.axis_size("outer")
    length, depth = tokens.shape
    local, xbc = w_in.shape
    block = max(local, 128)
    tail_rows = 16
    dt_block = w_dt.T
    if block != local:
        start = lax.rem(lax.axis_index("inner") * local, block)
        dt_block = lax.dynamic_update_slice(
            jnp.zeros((HEADS, block), BF16), dt_block, (jnp.int32(0), start)
        )
    streams = xbc // 4 // 128
    dma = pltpu.SemaphoreType.DMA
    vmem = pl.BlockSpec(memory_space=pltpu.VMEM)
    whole = pl.BlockSpec(memory_space=pl.ANY)
    return pl.pallas_call(
        partial(project_kernel, n, n_out),
        out_shape=(
            jax.ShapeDtypeStruct((length, xbc), BF16),
            jax.ShapeDtypeStruct((tail_rows, xbc), BF16),
            jax.ShapeDtypeStruct((length, HEADS), BF16),
        ),
        in_specs=[whole, whole, vmem],
        out_specs=(vmem, vmem, vmem),
        scratch_shapes=[
            pltpu.VMEM((length + tail_rows, depth), BF16),
            pltpu.VMEM((2, depth, xbc // 2), BF16),
            pltpu.VMEM((xbc // 256, length + tail_rows, 256), F32),
            pltpu.VMEM((n, HEADS, block), BF16),
            dma((2, streams, n)), dma((2, streams, n)),
            dma((2, streams, n)), dma((2, streams, n)),
            dma((2, streams, n)), dma((2, streams, n)),
            dma((n,)), dma((n,)), dma((3,)), dma(()), dma(()),
        ],
        compiler_params=pltpu.CompilerParams(
            collective_id=2, has_side_effects=True, vmem_limit_bytes=60 * 2**20
        ),
        name="project",
    )(tokens, w_in, dt_block)


def per_device(tokens, w_in, w_dt, conv_w, conv_b, dt_bias, a_log, d_skip, norm_gain):
    own_rows = tokens.reshape(tokens.shape[1], tokens.shape[2])
    row_count = own_rows.shape[0]
    projected, tail, dt_raw = run_project(own_rows, w_in, w_dt)
    mixed, entry = run_scan(
        projected, tail, dt_raw, conv_w, conv_b, dt_bias, a_log, d_skip, norm_gain
    )
    return (
        mixed.reshape(1, row_count, HP),
        entry.reshape(1, 1, HEADS, P_SIZE, N),
    )


def solution(mesh):
    placed = (
        P(("grp", "outer"), "inner", None),
        P("inner", None),
        P("inner", None),
        P(), P(), P(), P(), P(), P(),
    )
    return jax.shard_map(
        per_device,
        mesh=mesh,
        in_specs=placed,
        out_specs=(
            P(("grp", "outer"), "inner", None),
            P(("grp", "outer"), "inner", None, None, None),
        ),
        check_vma=False,
    )
```
